256 devices in a mesh: chan: 8 (over z), ctx: 32 (over x, y, core).
Axes of the slice: x: 4, y: 4, z: 8, core: 2. Of those that a mesh axis runs over, the one named last changes fastest.
Arguments:
- projected: bfloat16 [32, 1024, 3, 4096], P('ctx', 'chan'), may hold values from -6 to 6
- short_taps: bfloat16 [3, 3, 4096], replicated, may hold values from -3 to 3
- long_filter: float32 [32768, 16], P('ctx', 'chan'), may hold values from -0.03125 to 0.03125
- skip_gain: float32 [4096], P('chan'), may hold values from -4 to 4
Outputs:
- gated: bfloat16 [32768, 4096], P('ctx', 'chan')
The draws below stay inside these ranges and needn't reach their ends.
All inputs are finite; a program needn't handle non-finite values.
Results may differ from the reference program's by a relative error of at most 0.0064.
Values may be sent and summed in bfloat16 or wider, within the bound.
No kernel may reach another device: no remote copies, remote signals or barrier semaphores. Data moves between devices by JAX's collectives and lax.ppermute only.
A program may use at most 128 MiB of HBM per device.

```python
import jax
import jax.numpy as jnp
from jax import lax

DW = 4096
GROUP = 256
TAPS = 3
BLOCK = 1024
LEN = 32768
GROUPS = 16
N_CTX = 32


def block_scale(rng, shape, shards, smallest, high):
    factor_of, own = 1.0, jax.random.fold_in(rng, 6)
    for position, parts in shards:
        draws = jnp.exp(jax.random.uniform(jax.random.fold_in(own, position), (parts,), jnp.float32, smallest / len(shards), high / len(shards)))
        factor_of = factor_of * jnp.repeat(draws, shape[position] // parts).reshape([-1 if axis == position else 1 for axis in range(len(shape))])
    return factor_of


def scatter_about(rng, dims, spread, bound, cuts=(), held_as=jnp.bfloat16):
    values = spread * jax.random.normal(rng, dims, jnp.float32)
    if cuts:
        values = values * block_scale(rng, dims, cuts, -0.22, 0.18)
    return jnp.clip(values, -bound, bound).astype(held_as)


def setup_inputs(seed: int = 0) -> dict:
    streams_of = jax.random.split(jax.random.key(seed), 5)
    projected = scatter_about(streams_of[0], (N_CTX, BLOCK, 3, DW), 1.0, 6.0, ((0, 32), (1, 8)))
    short_taps = scatter_about(streams_of[1], (TAPS, 3, DW), 0.6, 3.0)
    long_filter = scatter_about(streams_of[2], (LEN, GROUPS), LEN ** -0.5, 0.03125, ((0, 32), (1, 8)), jnp.float32)
    skip_gain = scatter_about(streams_of[3], (DW,), 1.0, 4.0, ((0, 8),), jnp.float32)
    return dict(projected=projected, short_taps=short_taps, long_filter=long_filter, skip_gain=skip_gain)


def stored(values):
    return lax.optimization_barrier(values.astype(jnp.bfloat16))


def reference(projected, short_taps, long_filter, skip_gain):
    flat = projected.reshape(LEN, 3, DW)

    def one_group(group_id):
        first_col = group_id * GROUP
        columns = lax.dynamic_slice_in_dim(flat, first_col, GROUP, 2).astype(jnp.float32)
        weights = lax.dynamic_slice_in_dim(short_taps, first_col, GROUP, 2).astype(jnp.float32)
        padded = jnp.pad(columns, ((TAPS - 1, 0), (0, 0), (0, 0)))
        summed = weights[0] * padded[TAPS - 1:TAPS - 1 + LEN]
        for offset in range(1, TAPS):
            summed = summed + weights[offset] * padded[TAPS - 1 - offset:TAPS - 1 - offset + LEN]
        queries = stored(summed[:, 0]).astype(jnp.float32)
        product = stored(summed[:, 1] * summed[:, 2]).astype(jnp.float32)
        kernel = lax.dynamic_index_in_dim(long_filter, group_id, 1, keepdims=False)
        spectrum = jnp.fft.rfft(product, n=2 * LEN, axis=0) * jnp.fft.rfft(kernel, n=2 * LEN)[:, None]
        convolved = jnp.fft.irfft(spectrum, n=2 * LEN, axis=0)[:LEN]
        gains = lax.dynamic_slice_in_dim(skip_gain, first_col, GROUP, 0)
        mixed = stored(convolved + gains * product).astype(jnp.float32)
        return (queries * mixed).astype(jnp.bfloat16)

    blocks = lax.map(one_group, jnp.arange(GROUPS, dtype=jnp.int32))
    return jnp.transpose(blocks, (1, 0, 2)).reshape(LEN, DW)
```

```python
import jax
import jax.numpy as jnp
from jax import lax
from jax.experimental import pallas as pl
from jax.experimental.pallas import tpu as pltpu
from jax.sharding import PartitionSpec as P


F32 = jnp.float32
BF16 = jnp.bfloat16
TILE = 128
GROUP_DEPTH = 8
ROW_CHUNK = 512
BIG = pltpu.CompilerParams(vmem_limit_bytes=60 * 1024 * 1024)
WHOLE = pl.BlockSpec(memory_space=pltpu.VMEM)


def estimate(flops, moved):
    return pl.CostEstimate(flops=flops, bytes_accessed=moved, transcendentals=0)


def featurize_kernel(x_ref, before_ref, taps_ref, query_ref, kv_ref):
    taps, _, columns = taps_ref.shape
    rows = x_ref.shape[1]
    index = lax.broadcasted_iota(jnp.int32, (rows, columns), 0)

    def feature(which):
        own = x_ref[which].astype(F32)
        before = before_ref[which].astype(F32)
        weights = taps_ref[:, which].astype(F32)
        total = weights[0:1] * own
        for lag in range(1, taps):
            moved = pltpu.roll(own, lag, 0)
            for row in range(lag):
                source = taps - 1 - lag + row
                moved = jnp.where(index == row, before[source : source + 1], moved)
            total = total + weights[lag : lag + 1] * moved
        return total

    query_ref[0] = feature(0).astype(BF16)
    product = feature(1) * feature(2)
    kv_ref[...] = product.T.astype(BF16).reshape(kv_ref.shape)


def featurize(own, before, taps, slots, per_device):
    streams, rows, channels = own.shape
    lags = taps.shape[0]
    columns = channels // slots
    pieces = columns // per_device
    return pl.pallas_call(
        featurize_kernel,
        grid=(slots,),
        out_shape=(
            jax.ShapeDtypeStruct((slots, rows, columns), BF16),
            jax.ShapeDtypeStruct((slots * pieces, per_device, rows), BF16),
        ),
        in_specs=[
            pl.BlockSpec((streams, rows, columns), lambda i: (0, 0, i)),
            pl.BlockSpec((streams, lags - 1, columns), lambda i: (0, 0, i)),
            pl.BlockSpec((lags, streams, columns), lambda i: (0, 0, i)),
        ],
        out_specs=(
            pl.BlockSpec((1, rows, columns), lambda i: (i, 0, 0)),
            pl.BlockSpec((pieces, per_device, rows), lambda i: (i, 0, 0)),
        ),
        cost_estimate=estimate(20 * own.size, 4 * own.size),
        name="featurize",
    )(own, before, taps)


def toeplitz_kernel(lags_ref, out_ref):
    count, tile = lags_ref.shape
    unroll = 8
    upper = lax.broadcasted_iota(jnp.int32, (tile, tile), 1) >= lax.broadcasted_iota(
        jnp.int32, (tile, tile), 0
    )
    zeros = jnp.zeros((tile, tile), F32)
    out_ref[0:tile, :] = zeros.astype(BF16)

    def step(index, earlier):
        first = pl.multiple_of(index * unroll, unroll)
        lines = lags_ref[pl.ds(first, unroll), :].astype(F32)
        for part in range(unroll):
            spread = jnp.broadcast_to(lines[part : part + 1], (tile, tile))
            turned = pltpu.roll(spread, 0, 1, stride=1, stride_axis=0)
            place = pl.multiple_of((first + part + 1) * tile, tile)
            out_ref[pl.ds(place, tile), :] = jnp.where(upper, turned, earlier).astype(BF16)
            earlier = turned
        return earlier

    lax.fori_loop(0, count // unroll, step, zeros)


def toeplitz(lags):
    count, tile = lags.shape
    size = (count + 1) * tile
    return pl.pallas_call(
        toeplitz_kernel,
        out_shape=jax.ShapeDtypeStruct((size, tile), BF16),
        in_specs=[WHOLE],
        out_specs=WHOLE,
        compiler_params=BIG,
        cost_estimate=estimate(4 * size * tile, 2 * size * tile),
        name="toeplitz",
    )(lags)


def convolve_kernel(x_ref, weights_ref, gain_ref, out_ref, wide_ref, total_ref):
    slots, devices, channels, tile = x_ref.shape
    pairs = slots * devices // 2
    depth = wide_ref.shape[1]
    taken = depth // tile
    group = taken // 2
    for part in range(taken):
        lanes = slice(part * tile, (part + 1) * tile)
        for pair in range(pairs):
            rows = slice(pair * channels, (pair + 1) * channels)
            block = 2 * pair + 1 - part
            if block < 0:
                wide_ref[rows, lanes] = jnp.zeros((channels, tile), BF16)
            else:
                wide_ref[rows, lanes] = x_ref[block % slots, block // slots]
    total_ref[...] = jnp.zeros_like(total_ref)
    height = pairs * channels
    stride = group * channels

    def step(index, carry):
        base = pl.multiple_of(index * depth, depth)
        next_base = pl.multiple_of(base + tile, tile)
        weights = jnp.concatenate(
            [weights_ref[pl.ds(base, depth), :], weights_ref[pl.ds(next_base, depth), :]], axis=1
        )
        chunks = (height - index * stride + ROW_CHUNK - 1) // ROW_CHUNK

        def rows_step(chunk, inner):
            source = pl.multiple_of(chunk * ROW_CHUNK, ROW_CHUNK)
            target = pl.ds(pl.multiple_of(source + index * stride, stride), ROW_CHUNK)
            total_ref[target, :] += jnp.dot(
                wide_ref[pl.ds(source, ROW_CHUNK), :], weights, preferred_element_type=F32
            )
            return inner

        return lax.fori_loop(0, chunks, rows_step, carry)

    lax.fori_loop(0, pairs // group, step, 0)
    gain = gain_ref[...]
    for block in range(2 * pairs):
        half = slice((block % 2) * tile, (block % 2 + 1) * tile)
        rows = slice((block // 2) * channels, (block // 2 + 1) * channels)
        direct = gain * x_ref[block % slots, block // slots].astype(F32)
        out_ref[block] = (total_ref[rows, half] + direct).astype(BF16)


def convolve(x, weights, gain):
    slots, devices, channels, tile = x.shape
    blocks = slots * devices
    height = blocks // 2 * channels
    depth = 2 * GROUP_DEPTH * tile
    return pl.pallas_call(
        convolve_kernel,
        out_shape=jax.ShapeDtypeStruct((blocks, channels, tile), BF16),
        in_specs=[WHOLE] * 3,
        out_specs=WHOLE,
        scratch_shapes=[
            pltpu.VMEM((height, depth), BF16),
            pltpu.VMEM((height + ROW_CHUNK, 2 * tile), F32),
        ],
        compiler_params=BIG,
        cost_estimate=estimate(blocks * blocks * channels * tile * tile, 4 * x.size + 2 * weights.size),
        name="convolve",
    )(x, weights, gain)


def gate_kernel(query_ref, mixed_ref, out_ref):
    columns = out_ref.shape[1]
    mixed = mixed_ref[:, 0].reshape(columns, -1).astype(F32)
    out_ref[...] = (query_ref[0].astype(F32) * mixed.T).astype(BF16)


def gate(query, mixed):
    slots, rows, columns = query.shape
    devices, _, channels, _ = mixed.shape
    return pl.pallas_call(
        gate_kernel,
        grid=(slots,),
        out_shape=jax.ShapeDtypeStruct((slots * rows, columns), BF16),
        in_specs=[
            pl.BlockSpec((1, rows, columns), lambda i: (i, 0, 0)),
            pl.BlockSpec((devices, 1, channels, rows), lambda i: (0, i, 0, 0)),
        ],
        out_specs=pl.BlockSpec((rows, columns), lambda i: (i, 0)),
        cost_estimate=estimate(2 * query.size, 6 * query.size),
        name="gate",
    )(query, mixed)


def stages(projected, short_taps, long_filter, skip_gain):
    devices = lax.axis_size("ctx")
    slots = lax.axis_size("chan")
    own = jnp.transpose(projected[0], (1, 0, 2))
    rows = own.shape[1]
    columns = skip_gain.shape[0]
    channels = columns // devices
    lags = short_taps.shape[0]

    order = [(t % slots) * devices + t // slots for t in range(slots * devices)]
    before = lax.ppermute(own[:, rows - (lags - 1) :], ("chan", "ctx"), list(zip(order, order[1:])))

    here = long_filter.shape[1]
    lines = jnp.repeat(long_filter.T.astype(BF16), devices // here, axis=0)
    lines = lines.reshape(devices, -1, TILE)
    lines = lax.all_to_all(lines, "ctx", 0, 0, tiled=True).reshape(-1, TILE)

    query, kv = featurize(own, before, short_taps, slots, channels)
    lines, kv = lax.optimization_barrier((lines, kv))
    weights = toeplitz(lines)
    kv = lax.all_to_all(kv, ("chan", "ctx"), 0, 0, tiled=True)
    query, kv = lax.optimization_barrier((query, kv))
    query = lax.all_to_all(query, "chan", 0, 0, tiled=True)

    gains = lax.dynamic_slice_in_dim(skip_gain, lax.axis_index("ctx") * channels, channels)
    gains = jnp.broadcast_to(gains[:, None], (channels, TILE))
    mixed = convolve(kv.reshape(slots, devices, channels, rows), weights, gains)
    mixed, query = lax.optimization_barrier((mixed, query))
    mixed = mixed.reshape(devices, slots, channels, rows)
    mixed = lax.all_to_all(mixed, "ctx", 0, 0, tiled=True)
    return gate(query, mixed)


def solution(mesh):
    placed = (P("ctx", "chan", None, None), P(), P("ctx", "chan"), P("chan"))
    return jax.shard_map(
        stages, mesh=mesh, in_specs=placed, out_specs=P("ctx", "chan"), check_vma=False
    )
```

```python
import functools

import jax
import jax.numpy as jnp
from jax import lax
from jax.experimental import pallas as pl
from jax.experimental.pallas import tpu as pltpu
from jax.sharding import PartitionSpec as P


F32 = jnp.float32
BF16 = jnp.bfloat16
TILE = 128
GROUP_DEPTH = 32
ROW_CHUNK = 512
BIG = pltpu.CompilerParams(vmem_limit_bytes=60 * 1024 * 1024)
WHOLE = pl.BlockSpec(memory_space=pltpu.VMEM)


def estimate(flops, moved):
    return pl.CostEstimate(flops=flops, bytes_accessed=moved, transcendentals=0)


def transposed(value):
    size = value.shape[1]
    ones = lax.broadcasted_iota(jnp.int32, (size, size), 0) == lax.broadcasted_iota(
        jnp.int32, (size, size), 1
    )
    return lax.dot_general(
        ones.astype(BF16), value, (((1,), (1,)), ((), ())), preferred_element_type=F32
    )


def featurize_kernel(here_ref, x_ref, before_ref, taps_ref, query_ref, kv_ref):
    taps, _, columns = taps_ref.shape
    rows = x_ref.shape[1]
    tile = 8
    index = lax.broadcasted_iota(jnp.int32, (tile, columns), 0)

    def feature(which):
        own = x_ref[which].astype(F32)
        before = before_ref[which].astype(F32)
        weights = taps_ref[:, which].astype(F32)
        total = weights[0:1] * own
        for lag in range(1, taps):
            moved = pltpu.roll(own, lag, 0)
            top = moved[:tile]
            for row in range(lag):
                source = taps - 1 - lag + row
                top = jnp.where(index == row, before[source : source + 1], top)
            moved = jnp.concatenate([top, moved[tile:]], axis=0)
            total = total + weights[lag : lag + 1] * moved
        return total

    query_ref[0] = feature(0).astype(BF16)
    product = (feature(1) * feature(2)).astype(BF16)
    _, per_device, _ = kv_ref.shape
    count = TILE // per_device
    for part in range(columns // TILE):
        turned = transposed(product[:, part * TILE : (part + 1) * TILE]).astype(BF16)
        kv_ref[part * count : (part + 1) * count] = turned.reshape(count, per_device, rows)


def featurize(here, own, before, taps, slots, per_device):
    streams, rows, channels = own.shape
    lags = taps.shape[0]
    columns = channels // slots
    pieces = columns // per_device
    return pl.pallas_call(
        featurize_kernel,
        grid_spec=pltpu.PrefetchScalarGridSpec(
            num_scalar_prefetch=1,
            grid=(slots,),
            in_specs=[
                pl.BlockSpec((streams, rows, columns), lambda i, here: (0, 0, i)),
                pl.BlockSpec((streams, lags - 1, columns), lambda i, here: (0, 0, i)),
                pl.BlockSpec((lags, streams, columns), lambda i, here: (0, 0, i)),
            ],
            out_specs=(
                pl.BlockSpec(
                    (1, rows, columns), lambda i, here: ((i + slots - here[0]) % slots, 0, 0)
                ),
                pl.BlockSpec((pieces, per_device, rows), lambda i, here: (i, 0, 0)),
            ),
        ),
        out_shape=(
            jax.ShapeDtypeStruct((slots, rows, columns), BF16),
            jax.ShapeDtypeStruct((slots * pieces, per_device, rows), BF16),
        ),
        cost_estimate=estimate(20 * own.size, 4 * own.size),
        name="featurize",
    )(here, own, before, taps)


def toeplitz_kernel(lags_ref, out_ref):
    count, tile = lags_ref.shape
    unroll = 8
    upper = lax.broadcasted_iota(jnp.int32, (tile, tile), 1) >= lax.broadcasted_iota(
        jnp.int32, (tile, tile), 0
    )
    zeros = jnp.zeros((tile, tile), F32)
    out_ref[0:tile, :] = zeros.astype(BF16)

    def step(index, earlier):
        first = pl.multiple_of(index * unroll, unroll)
        lines = lags_ref[pl.ds(first, unroll), :].astype(F32)
        for part in range(unroll):
            spread = jnp.broadcast_to(lines[part : part + 1], (tile, tile))
            turned = pltpu.roll(spread, 0, 1, stride=1, stride_axis=0)
            place = pl.multiple_of((first + part + 1) * tile, tile)
            out_ref[pl.ds(place, tile), :] = jnp.where(upper, turned, earlier).astype(BF16)
            earlier = turned
        return earlier

    lax.fori_loop(0, count // unroll, step, zeros)


def toeplitz(lags):
    count, tile = lags.shape
    size = (count + 1) * tile
    return pl.pallas_call(
        toeplitz_kernel,
        out_shape=jax.ShapeDtypeStruct((size, tile), BF16),
        in_specs=[WHOLE],
        out_specs=WHOLE,
        compiler_params=BIG,
        cost_estimate=estimate(4 * size * tile, 2 * size * tile),
        name="toeplitz",
    )(lags)


def convolve_kernel(x_ref, weights_ref, gain_ref, out_ref, pair_ref, total_ref, *, margin, group):
    slots, devices, channels, tile = x_ref.shape
    pairs = slots * devices // 2
    pair_ref[0:margin, :] = jnp.zeros((margin, 2 * tile), BF16)
    for pair in range(pairs):
        start = margin + pair * channels
        for half in range(2):
            block = 2 * pair + 1 - half
            lanes = slice(half * tile, (half + 1) * tile)
            pair_ref[start : start + channels, lanes] = x_ref[block % slots, block // slots]
    depth = 2 * group * tile
    stride = group * channels
    gain = gain_ref[...]
    for top in range(0, pairs * channels, ROW_CHUNK):

        def step(index, carry, top=top):
            base = pl.multiple_of(index * depth, depth)
            next_base = pl.multiple_of(base + tile, tile)
            weights = jnp.concatenate(
                [weights_ref[pl.ds(base, depth), :], weights_ref[pl.ds(next_base, depth), :]],
                axis=1,
            )
            parts = []
            for part in range(group):
                start = pl.multiple_of(margin + top - index * stride - part * channels, channels)
                parts.append(pair_ref[pl.ds(start, ROW_CHUNK), :])
            total_ref[...] += jnp.dot(
                jnp.concatenate(parts, axis=1), weights, preferred_element_type=F32
            )
            return carry

        total_ref[...] = jnp.zeros_like(total_ref)
        lax.fori_loop(0, (top + ROW_CHUNK + stride - 1) // stride, step, 0)
        for pair in range(ROW_CHUNK // channels):
            rows = slice(pair * channels, (pair + 1) * channels)
            for half in range(2):
                block = 2 * (top // channels + pair) + half
                lanes = slice(half * tile, (half + 1) * tile)
                direct = gain * x_ref[block % slots, block // slots].astype(F32)
                out_ref[block] = (total_ref[rows, lanes] + direct).astype(BF16)


def convolve(x, weights, gain):
    slots, devices, channels, tile = x.shape
    blocks = slots * devices
    height = blocks // 2 * channels
    margin = max(GROUP_DEPTH * channels, ROW_CHUNK)
    return pl.pallas_call(
        functools.partial(convolve_kernel, margin=margin, group=GROUP_DEPTH),
        out_shape=jax.ShapeDtypeStruct((blocks, channels, tile), BF16),
        in_specs=[WHOLE] * 3,
        out_specs=WHOLE,
        scratch_shapes=[
            pltpu.VMEM((height + margin, 2 * tile), BF16),
            pltpu.VMEM((ROW_CHUNK, 2 * tile), F32),
        ],
        compiler_params=BIG,
        cost_estimate=estimate(blocks * blocks * channels * tile * tile, 4 * x.size + 2 * weights.size),
        name="convolve",
    )(x, weights, gain)


def gate_kernel(here_ref, *refs):
    queries, mixed_ref, out_ref = refs[:-2], refs[-2], refs[-1]
    slots = len(queries)
    rows, columns = queries[0].shape
    for shift, query_ref in enumerate(queries):
        slot = (here_ref[0] + slots - shift) % slots
        mixed = mixed_ref[:, pl.ds(slot, 1)].reshape(columns, rows)
        target = pl.ds(pl.multiple_of(slot * rows, rows), rows)
        out_ref[target, :] = (query_ref[...].astype(F32) * transposed(mixed)).astype(BF16)


def gate(here, queries, mixed):
    rows, columns = queries[0].shape
    total = len(queries) * rows
    return pl.pallas_call(
        gate_kernel,
        out_shape=jax.ShapeDtypeStruct((total, columns), BF16),
        in_specs=[pl.BlockSpec(memory_space=pltpu.SMEM)] + [WHOLE] * (len(queries) + 1),
        out_specs=WHOLE,
        compiler_params=pltpu.CompilerParams(vmem_limit_bytes=16 * 1024 * 1024),
        cost_estimate=estimate(2 * total * columns, 6 * total * columns),
        name="gate",
    )(here, *queries, mixed)


def stages(projected, short_taps, long_filter, skip_gain):
    devices = lax.axis_size("ctx")
    slots = lax.axis_size("chan")
    own = jnp.transpose(projected[0], (1, 0, 2))
    rows = own.shape[1]
    columns = skip_gain.shape[0]
    channels = columns // devices
    lags = short_taps.shape[0]
    here = lax.axis_index("chan").astype(jnp.int32).reshape(1)

    order = [(t % slots) * devices + t // slots for t in range(slots * devices)]
    pairs = list(zip(order, order[1:]))
    before = lax.ppermute(own[:, rows - (lags - 1) :], ("chan", "ctx"), pairs)

    groups = long_filter.shape[1]
    lines = jnp.repeat(long_filter.T.astype(BF16), devices // groups, axis=0)
    lines = lines.reshape(devices, -1, TILE)
    lines = lax.all_to_all(lines, "ctx", 0, 0, tiled=True).reshape(-1, TILE)

    query, kv = featurize(here, own, before, short_taps, slots, channels)
    lines, kv = lax.optimization_barrier((lines, kv))
    weights = toeplitz(lines)
    kv = lax.all_to_all(kv, ("chan", "ctx"), 0, 0, tiled=True)
    queries = [query[0]]
    for shift in range(1, slots):
        ring = [(i, (i + shift) % slots) for i in range(slots)]
        queries.append(lax.ppermute(query[shift], "chan", ring))

    gains = lax.dynamic_slice_in_dim(skip_gain, lax.axis_index("ctx") * channels, channels)
    gains = jnp.broadcast_to(gains[:, None], (channels, TILE))
    mixed = convolve(kv.reshape(slots, devices, channels, rows), weights, gains)
    mixed = mixed.reshape(devices, slots, channels, rows)
    mixed = lax.all_to_all(mixed, "ctx", 0, 0, tiled=True)
    return gate(here, queries, mixed)


def solution(mesh):
    placed = (P("ctx", "chan", None, None), P(), P("ctx", "chan"), P("chan"))
    return jax.shard_map(
        stages, mesh=mesh, in_specs=placed, out_specs=P("ctx", "chan"), check_vma=False
    )
```

```python
import jax
import jax.numpy as jnp
from jax import lax
from jax.experimental import pallas as pl
from jax.experimental.pallas import tpu as pltpu
from jax.sharding import PartitionSpec as P


F32 = jnp.float32
BF16 = jnp.bfloat16
TILE = 128
ROW_CHUNK = 512
SPLIT = 4
MIB = 1024 * 1024
SMALL = pltpu.CompilerParams(vmem_limit_bytes=16 * MIB)
LARGE = pltpu.CompilerParams(vmem_limit_bytes=58 * MIB)
WIDE = pltpu.CompilerParams(vmem_limit_bytes=62 * MIB)
WHOLE = pl.BlockSpec(memory_space=pltpu.VMEM)
FAR = pl.BlockSpec(memory_space=pltpu.HBM)
SCALARS = pl.BlockSpec(memory_space=pltpu.SMEM)


def estimate(flops, moved):
    return pl.CostEstimate(flops=flops, bytes_accessed=moved, transcendentals=0)


def identity(size):
    rows = lax.broadcasted_iota(jnp.int32, (size, size), 0)
    return (rows == lax.broadcasted_iota(jnp.int32, (size, size), 1)).astype(BF16)


def transposed(value, ones):
    return lax.dot_general(ones, value, (((1,), (1,)), ((), ())), preferred_element_type=F32)


def featurize_kernel(
    here_ref, own_ref, before_ref, taps_ref, query_ref, kv_ref, x_ref, rows_ref, made_ref, sent_ref, arrived, left
):
    taps, streams, _ = taps_ref.shape
    slots, rows, columns = made_ref.shape
    pieces, per_device = sent_ref.shape[1:3]
    lead = rows_ref.shape[1] - rows
    parts = columns // TILE
    count = TILE // per_device
    earlier = taps - 1
    ones = identity(TILE)

    def fetch(which):
        return pltpu.make_async_copy(own_ref.at[which], x_ref.at[which], arrived.at[which])

    def leave(slot):
        turn = (slot + slots - here_ref[0]) % slots
        first = pl.multiple_of(slot * pieces, pieces)
        return (
            pltpu.make_async_copy(made_ref.at[slot], query_ref.at[turn], left.at[0, slot]),
            pltpu.make_async_copy(
                sent_ref.at[slot], kv_ref.at[pl.ds(first, pieces)], left.at[1, slot]
            ),
        )

    for which in range(streams):
        fetch(which).start()
    for which in range(streams):
        fetch(which).wait()

    def step(slot, carry):
        for part in range(parts):
            lanes = slice(part * TILE, (part + 1) * TILE)
            along = pl.ds(pl.multiple_of(slot * columns + part * TILE, TILE), TILE)

            def feature(which):
                slab = which * parts + part
                rows_ref[slab, lead:, :] = x_ref[which, :, along].astype(F32)
                rows_ref[slab, lead - earlier : lead, :] = before_ref[which, :, along].astype(F32)
                weights = taps_ref[:, which, along].astype(F32)
                total = weights[0:1] * rows_ref[slab, lead:, :]
                for lag in range(1, taps):
                    moved = rows_ref[slab, lead - lag : lead - lag + rows, :]
                    total = total + weights[lag : lag + 1] * moved
                return total

            made_ref[slot, :, lanes] = feature(0).astype(BF16)
            product = (feature(1) * feature(2)).astype(BF16)
            turned = transposed(product, ones).astype(BF16)
            sent_ref[slot, part * count : (part + 1) * count] = turned.reshape(
                count, per_device, rows
            )
        for copy in leave(slot):
            copy.start()
        return carry

    lax.fori_loop(0, slots, step, 0)
    for slot in range(slots):
        for copy in leave(slot):
            copy.wait()


def featurize(here, own, before, taps, slots, per_device):
    streams, rows, channels = own.shape
    columns = channels // slots
    pieces = columns // per_device
    return pl.pallas_call(
        featurize_kernel,
        out_shape=(
            jax.ShapeDtypeStruct((slots, rows, columns), BF16),
            jax.ShapeDtypeStruct((slots * pieces, per_device, rows), BF16),
        ),
        in_specs=[SCALARS, FAR, WHOLE, WHOLE],
        out_specs=(FAR, FAR),
        scratch_shapes=[
            pltpu.VMEM((streams, rows, channels), BF16),
            pltpu.VMEM((streams * columns // TILE, rows + 8, TILE), F32),
            pltpu.VMEM((slots, rows, columns), BF16),
            pltpu.VMEM((slots, pieces, per_device, rows), BF16),
            pltpu.SemaphoreType.DMA((streams,)),
            pltpu.SemaphoreType.DMA((2, slots)),
        ],
        compiler_params=WIDE,
        cost_estimate=estimate(20 * own.size, 4 * own.size),
        name="featurize",
    )(here, own, before, taps)


def toeplitz_kernel(lags_ref, out_ref, earlier_ref):
    count, tile = lags_ref.shape
    upper = lax.broadcasted_iota(jnp.int32, (tile, tile), 1) >= lax.broadcasted_iota(
        jnp.int32, (tile, tile), 0
    )

    @pl.when(pl.program_id(0) == 0)
    def _():
        earlier_ref[...] = jnp.zeros_like(earlier_ref)

    earlier = earlier_ref[...]
    lines = lags_ref[...].astype(F32)
    for part in range(count):
        spread = jnp.broadcast_to(lines[part : part + 1], (tile, tile))
        turned = pltpu.roll(spread, 0, 1, stride=1, stride_axis=0)
        place = slice(part * tile, (part + 1) * tile)
        out_ref[place, :] = jnp.where(upper, turned, earlier).astype(BF16)
        earlier = turned
    earlier_ref[...] = earlier


def toeplitz(lags):
    count, tile = lags.shape
    each = 16
    return pl.pallas_call(
        toeplitz_kernel,
        grid=(count // each,),
        out_shape=jax.ShapeDtypeStruct((count * tile, tile), BF16),
        in_specs=[pl.BlockSpec((each, tile), lambda i: (i, 0))],
        out_specs=pl.BlockSpec((each * tile, tile), lambda i: (i, 0)),
        scratch_shapes=[pltpu.VMEM((tile, tile), F32)],
        compiler_params=WIDE,
        cost_estimate=estimate(4 * count * tile * tile, 2 * count * tile * tile),
        name="toeplitz",
    )(lags)


def convolve_kernel(
    here_ref, gain_ref, x_ref, tiles_ref, out_ref, weights_ref, pair_ref, total_ref, made_ref, arrived, left
):
    slots, devices, channels, tile = x_ref.shape
    pairs = slots * devices // 2
    group = ROW_CHUNK // channels
    share = 2 * group * tile // SPLIT

    def fetch(index, piece):
        start = pl.multiple_of((index * SPLIT + piece) * share, share)
        kept = pl.multiple_of(start + tile, tile)
        return pltpu.make_async_copy(
            tiles_ref.at[pl.ds(start, share), :],
            weights_ref.at[pl.ds(kept, share), :],
            arrived.at[index, piece],
        )

    def leave(index):
        first = pl.ds(pl.multiple_of(index * (2 * group), 2 * group), 2 * group)
        return pltpu.make_async_copy(made_ref.at[first], out_ref.at[first], left.at[index])

    shares = pairs // group
    for piece in range(SPLIT):
        fetch(0, piece).start()
    weights_ref[0:tile, :] = jnp.zeros((tile, tile), BF16)
    part = group // SPLIT
    margin = part * channels
    pair_ref[0:margin, :] = jnp.zeros((margin, 2 * tile), BF16)
    for pair in range(pairs):
        start = margin + pair * channels
        for half in range(2):
            block = 2 * pair + 1 - half
            lanes = slice(half * tile, (half + 1) * tile)
            pair_ref[start : start + channels, lanes] = x_ref[block % slots, block // slots]
    channel = lax.broadcasted_iota(jnp.int32, (channels, tile), 0)
    gain = jnp.zeros((channels, tile), F32)
    for index in range(channels):
        gain = jnp.where(channel == index, gain_ref[here_ref[0] * channels + index], gain)

    def product(lag, count, starts, height):
        base = pl.multiple_of(lag * (2 * tile), 2 * tile)
        next_base = pl.multiple_of(base + tile, tile)
        depth = count * 2 * tile
        weights = jnp.concatenate(
            [weights_ref[pl.ds(base, depth), :], weights_ref[pl.ds(next_base, depth), :]], axis=1
        )
        rows = jnp.concatenate([pair_ref[pl.ds(start, height), :] for start in starts], axis=1)
        return jnp.dot(rows, weights, preferred_element_type=F32)

    def chunk(index, carry):
        for piece in range(SPLIT):
            fetch(index, piece).wait()

        @pl.when(index + 1 < shares)
        def _():
            for piece in range(SPLIT):
                fetch(index + 1, piece).start()

        top = pl.multiple_of(index * ROW_CHUNK, ROW_CHUNK)
        for piece in range(SPLIT):
            skipped = piece * margin
            starts = [margin - i * channels for i in range(part)]
            lag = index * group + piece * part
            value = product(lag, part, starts, ROW_CHUNK - skipped)
            if piece == 0:
                total_ref[...] = value
            else:
                total_ref[skipped:, :] += value

        def step(past, inner):
            first = margin + top - past * ROW_CHUNK
            starts = [pl.multiple_of(first - i * channels, channels) for i in range(group)]
            total_ref[...] += product(past * group, group, starts, ROW_CHUNK)
            return inner

        lax.fori_loop(0, index, step, 0)
        for pair in range(group):
            rows = slice(pair * channels, (pair + 1) * channels)
            for half in range(2):
                block = 2 * pair + half
                lanes = slice(half * tile, (half + 1) * tile)
                device = index * (2 * group // slots) + block // slots
                direct = gain * x_ref[block % slots, device].astype(F32)
                made_ref[index * (2 * group) + block] = (total_ref[rows, lanes] + direct).astype(BF16)
        leave(index).start()
        return carry

    lax.fori_loop(0, shares, chunk, 0)
    for index in range(shares):
        leave(index).wait()


def convolve(here, gain, x, weights):
    slots, devices, channels, tile = x.shape
    blocks = slots * devices
    height = blocks // 2 * channels
    return pl.pallas_call(
        convolve_kernel,
        out_shape=jax.ShapeDtypeStruct((blocks, channels, tile), BF16),
        in_specs=[SCALARS, SCALARS, WHOLE, FAR],
        out_specs=FAR,
        scratch_shapes=[
            pltpu.VMEM((weights.shape[0] + tile, tile), BF16),
            pltpu.VMEM((height + ROW_CHUNK // SPLIT, 2 * tile), BF16),
            pltpu.VMEM((ROW_CHUNK, 2 * tile), F32),
            pltpu.VMEM((blocks, channels, tile), BF16),
            pltpu.SemaphoreType.DMA((height // ROW_CHUNK, SPLIT)),
            pltpu.SemaphoreType.DMA((height // ROW_CHUNK,)),
        ],
        compiler_params=LARGE,
        cost_estimate=estimate(blocks * blocks * channels * tile * tile, 4 * x.size + 2 * weights.size),
        name="convolve",
    )(here, gain, x, weights)


def gate_kernel(here_ref, *refs):
    queries, mixed_ref, out_ref = refs[:-2], refs[-2], refs[-1]
    slots = len(queries)
    rows, columns = queries[0].shape
    ones = identity(rows)
    for shift, query_ref in enumerate(queries):
        slot = (here_ref[0] + slots - shift) % slots
        mixed = mixed_ref[:, pl.ds(slot, 1)].reshape(columns, rows)
        target = pl.ds(pl.multiple_of(slot * rows, rows), rows)
        out_ref[target, :] = (query_ref[...].astype(F32) * transposed(mixed, ones)).astype(BF16)


def gate(here, queries, mixed):
    rows, columns = queries[0].shape
    total = len(queries) * rows
    return pl.pallas_call(
        gate_kernel,
        out_shape=jax.ShapeDtypeStruct((total, columns), BF16),
        in_specs=[SCALARS] + [WHOLE] * (len(queries) + 1),
        out_specs=WHOLE,
        compiler_params=SMALL,
        cost_estimate=estimate(2 * total * columns, 6 * total * columns),
        name="gate",
    )(here, *queries, mixed)


def stages(projected, short_taps, long_filter, skip_gain):
    devices = lax.axis_size("ctx")
    slots = lax.axis_size("chan")
    own = jnp.transpose(projected[0], (1, 0, 2))
    rows = own.shape[1]
    columns = skip_gain.shape[0]
    channels = columns // devices
    lags = short_taps.shape[0]
    here = lax.axis_index("chan").astype(jnp.int32).reshape(1)

    order = [(t % slots) * devices + t // slots for t in range(slots * devices)]
    pairs = list(zip(order, order[1:]))
    before = lax.ppermute(own[:, rows - (lags - 1) :], ("chan", "ctx"), pairs)

    groups = long_filter.shape[1]
    lines = jnp.repeat(long_filter.T.astype(BF16), devices // groups, axis=0)
    lines = lines.reshape(devices, -1, TILE)
    lines = lax.all_to_all(lines, "ctx", 0, 0, tiled=True).reshape(-1, TILE)

    query, kv = featurize(here, own, before, short_taps, slots, channels)
    lines, kv = lax.optimization_barrier((lines, kv))
    weights = toeplitz(lines)
    kv = lax.all_to_all(kv, ("chan", "ctx"), 0, 0, tiled=True)
    queries = [query[0]]
    for shift in range(1, slots):
        ring = [(i, (i + shift) % slots) for i in range(slots)]
        queries.append(lax.ppermute(query[shift], "chan", ring))

    place = lax.axis_index("ctx").astype(jnp.int32).reshape(1)
    kv = kv.reshape(slots, devices, channels, rows)
    mixed = convolve(place, skip_gain, kv, weights)
    mixed = mixed.reshape(devices, slots, channels, rows)
    mixed = lax.all_to_all(mixed, "ctx", 0, 0, tiled=True)
    return gate(here, queries, mixed)


def solution(mesh):
    placed = (P("ctx", "chan", None, None), P(), P("ctx", "chan"), P("chan"))
    return jax.shard_map(
        stages, mesh=mesh, in_specs=placed, out_specs=P("ctx", "chan"), check_vma=False
    )
```

```python
import jax
import jax.numpy as jnp
from jax import lax
from jax.experimental import pallas as pl
from jax.experimental.pallas import tpu as pltpu
from jax.sharding import PartitionSpec as P


F32 = jnp.float32
BF16 = jnp.bfloat16
TILE = 128
ROW_CHUNK = 1024
SPLIT = 8
MIB = 1024 * 1024
SMALL = pltpu.CompilerParams(vmem_limit_bytes=16 * MIB)
LARGE = pltpu.CompilerParams(vmem_limit_bytes=58 * MIB)
WIDE = pltpu.CompilerParams(vmem_limit_bytes=62 * MIB)
WHOLE = pl.BlockSpec(memory_space=pltpu.VMEM)
FAR = pl.BlockSpec(memory_space=pltpu.HBM)
SCALARS = pl.BlockSpec(memory_space=pltpu.SMEM)


def estimate(flops, moved):
    return pl.CostEstimate(flops=flops, bytes_accessed=moved, transcendentals=0)


def identity(size):
    rows = lax.broadcasted_iota(jnp.int32, (size, size), 0)
    return (rows == lax.broadcasted_iota(jnp.int32, (size, size), 1)).astype(BF16)


def transposed(value, ones):
    return lax.dot_general(ones, value, (((1,), (1,)), ((), ())), preferred_element_type=F32)


def featurize_kernel(
    here_ref, own_ref, before_ref, taps_ref, query_ref, kv_ref, x_ref, rows_ref, made_ref, sent_ref, arrived, left
):
    taps, streams, _ = taps_ref.shape
    slots, rows, columns = made_ref.shape
    pieces, per_device = sent_ref.shape[1:3]
    lead = rows_ref.shape[1] - rows
    parts = columns // TILE
    count = TILE // per_device
    earlier = taps - 1
    ones = identity(TILE)

    share = own_ref.shape[2] // arrived.shape[1]

    def fetch(which, index):
        lanes = pl.ds(pl.multiple_of(index * share, share), share)
        return pltpu.make_async_copy(
            own_ref.at[which, :, lanes], x_ref.at[which, :, lanes], arrived.at[which, index]
        )

    def leave(slot):
        turn = (slot + slots - here_ref[0]) % slots
        first = pl.multiple_of(slot * pieces, pieces)
        return (
            pltpu.make_async_copy(made_ref.at[slot], query_ref.at[turn], left.at[0, slot]),
            pltpu.make_async_copy(
                sent_ref.at[slot], kv_ref.at[pl.ds(first, pieces)], left.at[1, slot]
            ),
        )

    for index in range(arrived.shape[1]):
        for which in range(streams):
            fetch(which, index).start()

    def step(slot, carry):
        @pl.when(slot * columns % share == 0)
        def _():
            for which in range(streams):
                fetch(which, slot * columns // share).wait()

        for part in range(parts):
            lanes = slice(part * TILE, (part + 1) * TILE)
            along = pl.ds(pl.multiple_of(slot * columns + part * TILE, TILE), TILE)

            def feature(which):
                slab = which * parts + part
                rows_ref[slab, lead:, :] = x_ref[which, :, along].astype(F32)
                rows_ref[slab, lead - earlier : lead, :] = before_ref[which, :, along].astype(F32)
                weights = taps_ref[:, which, along].astype(F32)
                total = weights[0:1] * rows_ref[slab, lead:, :]
                for lag in range(1, taps):
                    moved = rows_ref[slab, lead - lag : lead - lag + rows, :]
                    total = total + weights[lag : lag + 1] * moved
                return total

            made_ref[slot, :, lanes] = feature(0).astype(BF16)
            product = (feature(1) * feature(2)).astype(BF16)
            turned = transposed(product, ones).astype(BF16)
            sent_ref[slot, part * count : (part + 1) * count] = turned.reshape(
                count, per_device, rows
            )
        for copy in leave(slot):
            copy.start()
        return carry

    lax.fori_loop(0, slots, step, 0)
    for slot in range(slots):
        for copy in leave(slot):
            copy.wait()


def featurize(here, own, before, taps, slots, per_device):
    streams, rows, channels = own.shape
    columns = channels // slots
    pieces = columns // per_device
    return pl.pallas_call(
        featurize_kernel,
        out_shape=(
            jax.ShapeDtypeStruct((slots, rows, columns), BF16),
            jax.ShapeDtypeStruct((slots * pieces, per_device, rows), BF16),
        ),
        in_specs=[SCALARS, FAR, WHOLE, WHOLE],
        out_specs=(FAR, FAR),
        scratch_shapes=[
            pltpu.VMEM((streams, rows, channels), BF16),
            pltpu.VMEM((streams * columns // TILE, rows + 8, TILE), F32),
            pltpu.VMEM((slots, rows, columns), BF16),
            pltpu.VMEM((slots, pieces, per_device, rows), BF16),
            pltpu.SemaphoreType.DMA((streams, 4)),
            pltpu.SemaphoreType.DMA((2, slots)),
        ],
        compiler_params=WIDE,
        cost_estimate=estimate(20 * own.size, 4 * own.size),
        name="featurize",
    )(here, own, before, taps)


def toeplitz_kernel(lags_ref, out_ref, made_ref, left):
    batches = made_ref.shape[0]
    count, tile = lags_ref.shape
    each = count // batches
    upper = lax.broadcasted_iota(jnp.int32, (tile, tile), 1) >= lax.broadcasted_iota(
        jnp.int32, (tile, tile), 0
    )

    def leave(index):
        size = each * tile
        target = pl.ds(pl.multiple_of(index * size, size), size)
        return pltpu.make_async_copy(made_ref.at[index], out_ref.at[target, :], left.at[index])

    def step(index, earlier):
        lines = lags_ref[pl.ds(pl.multiple_of(index * each, each), each), :].astype(F32)
        for part in range(each):
            spread = jnp.broadcast_to(lines[part : part + 1], (tile, tile))
            turned = pltpu.roll(spread, 0, 1, stride=1, stride_axis=0)
            place = slice(part * tile, (part + 1) * tile)
            made_ref[index, place, :] = jnp.where(upper, turned, earlier).astype(BF16)
            earlier = turned
        leave(index).start()
        return earlier

    lax.fori_loop(0, batches, step, jnp.zeros((tile, tile), F32))
    for index in range(batches):
        leave(index).wait()


def toeplitz(lags):
    count, tile = lags.shape
    batches = count // 16
    return pl.pallas_call(
        toeplitz_kernel,
        out_shape=jax.ShapeDtypeStruct((count * tile, tile), BF16),
        in_specs=[WHOLE],
        out_specs=FAR,
        scratch_shapes=[
            pltpu.VMEM((batches, count // batches * tile, tile), BF16),
            pltpu.SemaphoreType.DMA((batches,)),
        ],
        compiler_params=WIDE,
        cost_estimate=estimate(4 * count * tile * tile, 2 * count * tile * tile),
        name="toeplitz",
    )(lags)


def convolve_kernel(
    here_ref, gain_ref, x_ref, tiles_ref, out_ref, weights_ref, pair_ref, total_ref, made_ref, arrived, left
):
    slots, devices, channels, tile = x_ref.shape
    pairs = slots * devices // 2
    group = ROW_CHUNK // channels
    share = 2 * group * tile // SPLIT

    def fetch(index, piece):
        start = pl.multiple_of((index * SPLIT + piece) * share, share)
        kept = pl.multiple_of(start + tile, tile)
        return pltpu.make_async_copy(
            tiles_ref.at[pl.ds(start, share), :],
            weights_ref.at[pl.ds(kept, share), :],
            arrived.at[index, piece],
        )

    def leave(index):
        first = pl.ds(pl.multiple_of(index * (2 * group), 2 * group), 2 * group)
        return pltpu.make_async_copy(made_ref.at[first], out_ref.at[first], left.at[index])

    shares = pairs // group
    for piece in range(SPLIT):
        fetch(0, piece).start()
    weights_ref[0:tile, :] = jnp.zeros((tile, tile), BF16)
    part = group // SPLIT
    margin = part * channels
    pair_ref[0:margin, :] = jnp.zeros((margin, 2 * tile), BF16)
    for pair in range(pairs):
        start = margin + pair * channels
        for half in range(2):
            block = 2 * pair + 1 - half
            lanes = slice(half * tile, (half + 1) * tile)
            pair_ref[start : start + channels, lanes] = x_ref[block % slots, block // slots]
    channel = lax.broadcasted_iota(jnp.int32, (channels, tile), 0)
    gain = jnp.zeros((channels, tile), F32)
    for index in range(channels):
        gain = jnp.where(channel == index, gain_ref[here_ref[0] * channels + index], gain)

    def product(lag, count, starts, height):
        base = pl.multiple_of(lag * (2 * tile), 2 * tile)
        next_base = pl.multiple_of(base + tile, tile)
        depth = count * 2 * tile
        weights = jnp.concatenate(
            [weights_ref[pl.ds(base, depth), :], weights_ref[pl.ds(next_base, depth), :]], axis=1
        )
        rows = jnp.concatenate([pair_ref[pl.ds(start, height), :] for start in starts], axis=1)
        return jnp.dot(rows, weights, preferred_element_type=F32)

    def chunk(index, carry):
        for piece in range(SPLIT):
            fetch(index, piece).wait()

        @pl.when(index + 1 < shares)
        def _():
            for piece in range(SPLIT):
                fetch(index + 1, piece).start()

        top = pl.multiple_of(index * ROW_CHUNK, ROW_CHUNK)
        for piece in range(SPLIT):
            skipped = piece * margin
            starts = [margin - i * channels for i in range(part)]
            lag = index * group + piece * part
            value = product(lag, part, starts, ROW_CHUNK - skipped)
            if piece == 0:
                total_ref[...] = value
            else:
                total_ref[skipped:, :] += value

        def step(past, inner):
            first = margin + top - past * ROW_CHUNK
            starts = [pl.multiple_of(first - i * channels, channels) for i in range(group)]
            total_ref[...] += product(past * group, group, starts, ROW_CHUNK)
            return inner

        lax.fori_loop(0, index, step, 0)
        for pair in range(group):
            rows = slice(pair * channels, (pair + 1) * channels)
            for half in range(2):
                block = 2 * pair + half
                lanes = slice(half * tile, (half + 1) * tile)
                device = index * (2 * group // slots) + block // slots
                direct = gain * x_ref[block % slots, device].astype(F32)
                made_ref[index * (2 * group) + block] = (total_ref[rows, lanes] + direct).astype(BF16)
        leave(index).start()
        return carry

    lax.fori_loop(0, shares, chunk, 0)
    for index in range(shares):
        leave(index).wait()


def convolve(here, gain, x, weights):
    slots, devices, channels, tile = x.shape
    blocks = slots * devices
    height = blocks // 2 * channels
    return pl.pallas_call(
        convolve_kernel,
        out_shape=jax.ShapeDtypeStruct((blocks, channels, tile), BF16),
        in_specs=[SCALARS, SCALARS, WHOLE, FAR],
        out_specs=FAR,
        scratch_shapes=[
            pltpu.VMEM((weights.shape[0] + tile, tile), BF16),
            pltpu.VMEM((height + ROW_CHUNK // SPLIT, 2 * tile), BF16),
            pltpu.VMEM((ROW_CHUNK, 2 * tile), F32),
            pltpu.VMEM((blocks, channels, tile), BF16),
            pltpu.SemaphoreType.DMA((height // ROW_CHUNK, SPLIT)),
            pltpu.SemaphoreType.DMA((height // ROW_CHUNK,)),
        ],
        compiler_params=LARGE,
        cost_estimate=estimate(blocks * blocks * channels * tile * tile, 4 * x.size + 2 * weights.size),
        name="convolve",
    )(here, gain, x, weights)


def gate_kernel(here_ref, *refs):
    queries, mixed_ref, out_ref = refs[:-2], refs[-2], refs[-1]
    slots = len(queries)
    rows, columns = queries[0].shape
    ones = identity(rows)
    for shift, query_ref in enumerate(queries):
        slot = (here_ref[0] + slots - shift) % slots
        mixed = mixed_ref[:, pl.ds(slot, 1)].reshape(columns, rows)
        target = pl.ds(pl.multiple_of(slot * rows, rows), rows)
        out_ref[target, :] = (query_ref[...].astype(F32) * transposed(mixed, ones)).astype(BF16)


def gate(here, queries, mixed):
    rows, columns = queries[0].shape
    total = len(queries) * rows
    return pl.pallas_call(
        gate_kernel,
        out_shape=jax.ShapeDtypeStruct((total, columns), BF16),
        in_specs=[SCALARS] + [WHOLE] * (len(queries) + 1),
        out_specs=WHOLE,
        compiler_params=SMALL,
        cost_estimate=estimate(2 * total * columns, 6 * total * columns),
        name="gate",
    )(here, *queries, mixed)


def stages(projected, short_taps, long_filter, skip_gain):
    devices = lax.axis_size("ctx")
    slots = lax.axis_size("chan")
    own = jnp.transpose(projected[0], (1, 0, 2))
    rows = own.shape[1]
    columns = skip_gain.shape[0]
    channels = columns // devices
    lags = short_taps.shape[0]
    here = lax.axis_index("chan").astype(jnp.int32).reshape(1)

    order = [(t % slots) * devices + t // slots for t in range(slots * devices)]
    pairs = list(zip(order, order[1:]))
    before = lax.ppermute(own[:, rows - (lags - 1) :], ("chan", "ctx"), pairs)

    groups = long_filter.shape[1]
    lines = jnp.repeat(long_filter.T.astype(BF16), devices // groups, axis=0)
    lines = lines.reshape(devices, -1, TILE)
    lines = lax.all_to_all(lines, "ctx", 0, 0, tiled=True).reshape(-1, TILE)

    query, kv = featurize(here, own, before, short_taps, slots, channels)
    lines, kv = lax.optimization_barrier((lines, kv))
    weights = toeplitz(lines)
    kv = lax.all_to_all(kv, ("chan", "ctx"), 0, 0, tiled=True)
    queries = [query[0]]
    for shift in range(1, slots):
        ring = [(i, (i + shift) % slots) for i in range(slots)]
        queries.append(lax.ppermute(query[shift], "chan", ring))

    place = lax.axis_index("ctx").astype(jnp.int32).reshape(1)
    kv = kv.reshape(slots, devices, channels, rows)
    mixed = convolve(place, skip_gain, kv, weights)
    mixed = mixed.reshape(devices, slots, channels, rows)
    mixed = lax.all_to_all(mixed, "ctx", 0, 0, tiled=True)
    return gate(here, queries, mixed)


def solution(mesh):
    placed = (P("ctx", "chan", None, None), P(), P("ctx", "chan"), P("chan"))
    return jax.shard_map(
        stages, mesh=mesh, in_specs=placed, out_specs=P("ctx", "chan"), check_vma=False
    )
```
